32 devices in a mesh: tiles: 2 (over y), sky: 4 (over x, core), visit: 4 (over z).
Axes of the slice: x: 2, y: 2, z: 4, core: 2. Of those that a mesh axis runs over, the one named last changes fastest.
Arguments:
- sky_model: float32 [512, 4096], P(('tiles', 'sky'), 'visit'), parts along dimension 0, may hold values from -6 to 6
- frames: bfloat16 [16, 128, 2048], P(('tiles', 'visit'), 'sky'), parts along dimension 0, may hold values from -8 to 8
- psf_rows: float32 [16, 5], P('tiles'), parts along dimension 0, may hold values from 0.1 to 1
- psf_cols: float32 [16, 5], P('tiles'), parts along dimension 0, may hold values from 0.1 to 1
- dither: int32 [16, 2], P('tiles'), parts along dimension 0, may hold values from -2 to 2
- footprint: int32 [16, 2], P('tiles'), parts along dimension 0, may hold values from 0 to 128, as said below
- huber_cut: float32 [16], P('tiles'), parts along dimension 0, may hold values from 0.3 to 1.5
Outputs:
- gradient: float32 [512, 4096], P(('tiles', 'sky'), 'visit'), parts along dimension 0
The draws below stay inside these ranges and needn't reach their ends.
There are 2 independent parts, one for each index of `tiles`. The reference program is written for one: setup_inputs(seed, part) draws one part's arguments, and reference() takes and returns one part's arrays. A program takes and returns all parts, laid end to end along the dimension named above; each array names one. Nothing has to cross between parts.
Inputs may be any that keep to these rules, and one draw needn't show every extreme that they name: `footprint`: each row is a visit's first covered frame row and one past its last, the first below the second; some visit starts at row 0 and some ends at row 128.
All inputs are finite; a program needn't handle non-finite values.
Results may differ from the reference program's by a relative error of at most 0.0003.
Values may be sent and summed in bfloat16 or wider, within the bound.
A program may use at most 128 MiB of HBM per device.

```python
import math
import jax
import jax.numpy as jnp
from jax import lax

TAPS = 5
H = 256
W = 4096
LH = 128
LW = 2048
K = 8


def draw_footprint(key, part):
    key_a, key_b, key_c, key_d = jax.random.split(jax.random.fold_in(key, 7), 4)
    first = jax.random.randint(key_a, (K,), 0, LH // 2)
    last = jax.random.randint(key_b, (K,), LH // 2 + 1, LH + 1)
    position = jnp.arange(K, dtype=jnp.int32)
    first = jnp.where(position == jax.random.randint(key_c, (), 0, K), 0, first)
    last = jnp.where(position == jax.random.randint(key_d, (), 0, K), LH, last)
    return jnp.stack([first, last], 1).astype(jnp.int32)


def plant(result, own_key, smallest, high):
    dims = result.shape
    spot = [jax.random.randint(jax.random.fold_in(own_key, axis), (), 0, dims[axis]) for axis in range(len(dims))]
    result = result.at[tuple(spot)].set(smallest)
    longest = dims.index(max(dims))
    spot[longest] = (spot[longest] + 1) % dims[longest]
    return result.at[tuple(spot)].set(high)


def level_of(key, extent, cuts, least, largest):
    def one(dim, shards_of):
        draws = jax.random.uniform(jax.random.fold_in(jax.random.fold_in(key, 6), dim), (shards_of,), jnp.float32, least / len(cuts), largest / len(cuts))
        return jnp.repeat(jnp.exp(draws), extent[dim] // shards_of).reshape((-1,) + (1,) * (len(extent) - dim - 1))

    factor_of = one(*cuts[0])
    for cut in cuts[1:]:
        factor_of = factor_of * one(*cut)
    return factor_of


def bell_draw(key, extent, width, reach, cuts=(), kind=jnp.bfloat16):
    values = width * jax.random.normal(key, extent, jnp.float32)
    if cuts:
        values = values * level_of(key, extent, cuts, -0.22, 0.18)
    return jnp.clip(values, -reach, reach).astype(kind)


def setup_inputs(seed: int = 0, part: int = 0) -> dict:
    splits = jax.random.split(jax.random.key(seed), 8)
    part_keys = jax.random.split(jax.random.fold_in(splits[7], part), 8)
    return {
        "sky_model": bell_draw(part_keys[0], (H, W), 1.0, 6.0, ((0, 4), (1, 4)), jnp.float32),
        "frames": bell_draw(part_keys[1], (K, LH, LW), 1.5, 8.0, ((0, 4), (1, 4))),
        "psf_rows": jnp.clip(jnp.exp(jax.random.uniform(part_keys[2], (K, TAPS), jnp.float32, math.log(0.1), math.log(1.0))), 0.1, 1.0),
        "psf_cols": jnp.clip(jnp.exp(jax.random.uniform(part_keys[3], (K, TAPS), jnp.float32, math.log(0.1), math.log(1.0))), 0.1, 1.0),
        "dither": plant(jax.random.randint(part_keys[4], (K, 2), -2, 3), jax.random.fold_in(part_keys[4], 1), -2, 2).astype(jnp.int32),
        "footprint": draw_footprint(jax.random.fold_in(jax.random.fold_in(splits[7], part), 71), part),
        "huber_cut": jnp.clip(jnp.exp(jax.random.uniform(part_keys[6], (K,), jnp.float32, math.log(0.3), math.log(1.5))), 0.3, 1.5),
    }


eps_flux = 0.1
tv_weight = 0.5
dither_bound = 2

def blur_down(values, offset, kernel, length, along_dim):
    half_taps = TAPS // 2
    margin = half_taps + dither_bound
    accum = None
    for b in range(TAPS):
        begin = offset + (b - half_taps + margin)
        piece = kernel[b] * lax.dynamic_slice_in_dim(values, begin, length, along_dim)
        accum = piece if accum is None else accum + piece
    if along_dim == 0:
        return accum[::2]
    return accum[:, ::2]

def spread_up(small, offset, kernel, extra, along_dim):
    half_taps = TAPS // 2
    margin = half_taps + dither_bound
    blank = jnp.zeros_like(small)
    if along_dim == 0:
        upsampled = jnp.stack([small, blank], 1).reshape(2 * small.shape[0], small.shape[1])
        padding = ((margin + extra, margin + extra), (0, 0))
    else:
        upsampled = jnp.stack([small, blank], 2).reshape(small.shape[0], 2 * small.shape[1])
        padding = ((0, 0), (margin + extra, margin + extra))
    padded = jnp.pad(upsampled, padding)
    length = upsampled.shape[along_dim] + 2 * extra
    accum = None
    for b in range(TAPS):
        begin = margin + half_taps - b - offset
        piece = kernel[b] * lax.dynamic_slice_in_dim(padded, begin, length, along_dim)
        accum = piece if accum is None else accum + piece
    return accum

def flux_divergence(window):
    grad_x = window[1:, :-1] - window[:-1, :-1]
    grad_y = window[:-1, 1:] - window[:-1, :-1]
    magnitude = jnp.sqrt(grad_x * grad_x + grad_y * grad_y + eps_flux)
    flux_u = grad_x / magnitude
    flux_w = grad_y / magnitude
    return flux_u[:-1, 1:] - flux_u[1:, 1:] + (flux_w[1:, :-1] - flux_w[1:, 1:])

def reference(sky_model, frames, psf_rows, psf_cols, dither, footprint, huber_cut):
    margin = TAPS // 2 + dither_bound
    padded = jnp.pad(sky_model, margin)
    low_index = jnp.arange(LH, dtype=jnp.int32)

    def one_visit(accum, k):
        row_shift = dither[k, 0]
        col_shift = dither[k, 1]
        columns = blur_down(padded, col_shift, psf_cols[k], W, 1)
        predicted = blur_down(columns, row_shift, psf_rows[k], H, 0)
        inside = (low_index >= footprint[k, 0]) & (low_index < footprint[k, 1])
        cutoff = huber_cut[k]
        clipped = jnp.where(inside[:, None], jnp.clip(predicted - frames[k].astype(jnp.float32), -cutoff, cutoff), jnp.zeros_like(predicted))
        back_rows = spread_up(clipped, row_shift, psf_rows[k], 0, 0)
        return (accum + spread_up(back_rows, col_shift, psf_cols[k], 0, 1), None)
    data_term, _ = lax.scan(one_visit, jnp.zeros((H, W), jnp.float32), jnp.arange(K, dtype=jnp.int32))
    window = jnp.pad(sky_model, 1)
    return data_term / jnp.sqrt(jnp.float32(K)) + tv_weight * flux_divergence(window)
```

```python
import functools

import jax
import jax.numpy as jnp
from jax import lax
from jax.experimental import pallas as pl
from jax.experimental.pallas import tpu as pltpu
from jax.sharding import PartitionSpec as P

TAPS = 5
REACH = 4
SHIFTS = 2 * REACH + 1

eps_flux = 0.1
tv_weight = 0.5

ROWS = 8
LANES = 128

NEIGHBOURS = tuple((y, x) for y in (-1, 0, 1) for x in (-1, 0, 1) if (y, x) != (0, 0))


def split_rows(value):
    high = value.astype(jnp.bfloat16)
    low = (value - high.astype(jnp.float32)).astype(jnp.bfloat16)
    return jnp.concatenate([high, low], axis=0)


def selection(shape, source_of):
    row = lax.broadcasted_iota(jnp.int32, shape, 0)
    col = lax.broadcasted_iota(jnp.int32, shape, 1)
    return jnp.where(source_of(row, col), 1.0, 0.0).astype(jnp.bfloat16)


def dot(a, b):
    return jnp.dot(a, b, preferred_element_type=jnp.float32)


def kernel(
    counts,
    model_ref,
    frames_ref,
    rows_ref,
    cols_ref,
    dither_ref,
    footprint_ref,
    cut_ref,
    out_ref,
    grid_ref,
    shifted_ref,
    frame_ref,
    blurred_ref,
    clipped_ref,
    back_ref,
    total_ref,
    whole_ref,
    side_ref,
    end_ref,
    corner_ref,
    local_sem,
    halo_send,
    halo_recv,
    frame_send,
    frame_recv,
    fold_send,
    fold_recv,
):
    sky_count, visit_count = counts
    height, width = out_ref.shape
    per_device, low_rows, low_cols = frame_ref.shape[1:]
    visits = rows_ref.shape[0]
    full_rows, full_cols = grid_ref.shape
    half_rows, half_cols = full_rows // 2, full_cols // 2
    blocks = full_cols // (2 * LANES)
    tile = lax.axis_index("tiles")
    sky = lax.axis_index("sky")
    visit = lax.axis_index("visit")

    def device(y, x):
        return (tile, sky + y, visit + x)

    def exists(y, x):
        ok = None
        for step, at, count in ((y, sky, sky_count), (x, visit, visit_count)):
            if step:
                here = at > 0 if step < 0 else at < count - 1
                ok = here if ok is None else ok & here
        return ok

    def peer_of(o):
        return lax.rem(visit + o, visit_count)

    def row_part(y):
        return (pl.ds(0, ROWS), pl.ds(ROWS, height), pl.ds(ROWS + height, ROWS))[y + 1]

    def col_part(x):
        return (pl.ds(width + LANES, LANES), pl.ds(0, width), pl.ds(width, LANES))[x + 1]

    def edge_of(y, x):
        r = (pl.ds(0, ROWS), pl.ds(0, height), pl.ds(height - ROWS, ROWS))[y + 1]
        c = (pl.ds(0, LANES), pl.ds(0, width), pl.ds(width - LANES, LANES))[x + 1]
        return r, c

    barrier = pltpu.get_barrier_semaphore()

    def greet(o, carry):
        pl.semaphore_signal(
            barrier, inc=1, device_id=(tile, sky, peer_of(o)), device_id_type=pl.DeviceIdType.MESH
        )
        return carry

    lax.fori_loop(1, visit_count, greet, 0)
    for y, x in NEIGHBOURS:
        if y:

            @pl.when(exists(y, x))
            def _():
                pl.semaphore_signal(
                    barrier, inc=1, device_id=device(y, x), device_id_type=pl.DeviceIdType.MESH
                )

    own_model = pltpu.make_async_copy(
        model_ref, grid_ref.at[pl.ds(ROWS, height), pl.ds(0, width)], local_sem.at[0]
    )
    own_model.start()

    def own_frames():
        return pltpu.make_async_copy(
            frames_ref.at[:, :, pl.ds(pl.multiple_of(visit * low_cols, low_cols), low_cols)],
            frame_ref.at[0],
            local_sem.at[1],
        )

    own_frames().start()

    up, down = (sky > 0).astype(jnp.int32), (sky < sky_count - 1).astype(jnp.int32)
    left, right = (visit > 0).astype(jnp.int32), (visit < visit_count - 1).astype(jnp.int32)
    pl.semaphore_wait(barrier, visit_count - 1 + (up + down) * (1 + left + right))

    def halo_copy(n, y, x):
        return pltpu.make_async_remote_copy(
            src_ref=model_ref.at[edge_of(y, x)],
            dst_ref=grid_ref.at[row_part(-y), col_part(-x)],
            send_sem=halo_send.at[n],
            recv_sem=halo_recv.at[n],
            device_id=device(y, x),
            device_id_type=pl.DeviceIdType.MESH,
        )

    def frame_copy(o):
        peer = peer_of(o)
        return pltpu.make_async_remote_copy(
            src_ref=frames_ref.at[:, :, pl.ds(pl.multiple_of(peer * low_cols, low_cols), low_cols)],
            dst_ref=frame_ref.at[o],
            send_sem=frame_send.at[o],
            recv_sem=frame_recv.at[o],
            device_id=(tile, sky, peer),
            device_id_type=pl.DeviceIdType.MESH,
        )

    for n, (y, x) in enumerate(NEIGHBOURS):

        @pl.when(exists(y, x))
        def _():
            halo_copy(n, y, x).start()

    def send_frames(o, carry):
        frame_copy(o).start()
        return carry

    lax.fori_loop(1, visit_count, send_frames, 0)

    for y, x in NEIGHBOURS:

        @pl.when(jnp.logical_not(exists(y, x)))
        def _():
            part = (row_part(y), col_part(x))
            grid_ref[part] = jnp.zeros(grid_ref.at[part].shape, jnp.float32)

    margin = (clipped_ref.shape[0] - low_rows) // 2
    clipped_ref[0:margin, :] = jnp.zeros((margin, low_cols), jnp.float32)
    clipped_ref[margin + low_rows :, :] = jnp.zeros((margin, low_cols), jnp.float32)
    total_ref[...] = jnp.zeros(total_ref.shape, jnp.float32)
    spread = selection(
        (2 * LANES, 2 * LANES),
        lambda a, b: a == jnp.where(b < LANES, 2 * b, 2 * b - (2 * LANES - 1)),
    )
    join = selection(
        (2 * LANES, 2 * LANES),
        lambda a, b: b == jnp.where(a < LANES, 2 * a, 2 * a - (2 * LANES - 1)),
    )

    def folded(b):
        return jnp.where(b >= full_rows, b - full_rows, b)

    part_rows = selection(
        (full_rows, 2 * full_rows),
        lambda a, b: folded(b) == jnp.where(a < half_rows, 2 * a, 2 * a - (full_rows - 1)),
    )
    join_rows = selection(
        (full_rows, 2 * full_rows),
        lambda a, b: a == jnp.where(folded(b) < half_rows, 2 * folded(b), 2 * folded(b) - (full_rows - 1)),
    )

    own_model.wait()
    for n, (y, x) in enumerate(NEIGHBOURS):
        @pl.when(exists(-y, -x))
        def _():
            halo_copy(n, y, x).wait_recv()

    for n in range(blocks):
        block = split_rows(grid_ref[:, 2 * LANES * n : 2 * LANES * (n + 1)])
        apart = dot(part_rows, dot(block, spread).astype(jnp.bfloat16))
        whole_ref[:, LANES * n : LANES * (n + 1)] = apart[:, :LANES]
        whole_ref[:, half_cols + LANES * n : half_cols + LANES * (n + 1)] = apart[:, LANES:]
    for d in range(SHIFTS):
        odd, step = (d - REACH) % 2, (d - REACH) // 2
        for p in range(2):
            value = whole_ref[half_rows * p : half_rows * (p + 1), half_cols * odd : half_cols * (odd + 1)]
            if step:
                value = pltpu.roll(value, (-step) % half_cols, 1)
            shifted_ref[d, p] = value[:, :low_cols]

    strip = 16

    def next_col(value):
        return pltpu.roll(value, full_cols - 1, 1)

    for t in range(height // strip):
        above = grid_ref[ROWS - 1 + strip * t : ROWS - 1 + strip * (t + 1), :]
        here = grid_ref[ROWS + strip * t : ROWS + strip * (t + 1), :]
        below = grid_ref[ROWS + 1 + strip * t : ROWS + 1 + strip * (t + 1), :]
        gx, gy = here - above, next_col(above) - above
        value = gx * lax.rsqrt(gx * gx + gy * gy + eps_flux)
        gx, gy = below - here, next_col(here) - here
        scale = lax.rsqrt(gx * gx + gy * gy + eps_flux)
        flux = gy * scale
        value = value - gx * scale + (pltpu.roll(flux, 1, 1) - flux)
        out_ref[strip * t : strip * (t + 1), :] = tv_weight * value[:, :width]

    own_frames().wait()
    low_index = sky * low_rows + lax.broadcasted_iota(jnp.int32, (low_rows, low_cols), 0)

    def taps(ref, k, offset):
        out = []
        for d in range(SHIFTS):
            at = d - REACH - offset + TAPS // 2
            value = ref[k, jnp.clip(at, 0, TAPS - 1)]
            out.append(jnp.where((at >= 0) & (at < TAPS), value, 0.0))
        return out

    def chunk(o, carry):
        @pl.when(o > 0)
        def _():
            frame_copy(o).wait_recv()

        owner = lax.rem(visit - o + visit_count, visit_count)
        col_taps = []
        for j in range(per_device):
            k = owner * per_device + j
            row_taps = taps(rows_ref, k, dither_ref[k, 0])
            col_shift = dither_ref[k, 1]
            col_taps.append(taps(cols_ref, k, col_shift))
            for p in range(2):
                value = None
                for b in range(TAPS):
                    piece = cols_ref[k, b] * shifted_ref[col_shift + (b - TAPS // 2 + REACH), p]
                    value = piece if value is None else value + piece
                blurred_ref[p] = value
            predicted = None
            for d in range(SHIFTS):
                odd, step = (d - REACH) % 2, (d - REACH) // 2
                begin = ROWS // 2 + step
                piece = row_taps[d] * blurred_ref[odd, begin : begin + low_rows, :]
                predicted = piece if predicted is None else predicted + piece
            cut = cut_ref[k]
            inside = (low_index >= footprint_ref[k, 0]) & (low_index < footprint_ref[k, 1])
            error = predicted - frame_ref[o, j].astype(jnp.float32)
            clipped_ref[margin : margin + low_rows, :] = jnp.where(
                inside, jnp.minimum(jnp.maximum(error, -cut), cut), 0.0
            )
            for p in range(2):
                value = None
                for d in range(SHIFTS):
                    odd, step = (d - REACH) % 2, (d - REACH) // 2
                    if odd == p:
                        begin = margin - ROWS // 2 - step
                        piece = row_taps[d] * clipped_ref[begin : begin + half_rows, :]
                        value = piece if value is None else value + piece
                back_ref[j, p] = value
        for p in range(2):
            for d in range(SHIFTS):
                value = total_ref[d, p, :, :low_cols]
                for j in range(per_device):
                    value = value + col_taps[j][d] * back_ref[j, p]
                total_ref[d, p, :, :low_cols] = value
        return carry

    lax.fori_loop(0, visit_count, chunk, 0)

    for odd in range(2):
        for p in range(2):
            value = None
            for d in range(SHIFTS):
                step = (d - REACH) // 2
                if (d - REACH) % 2 == odd:
                    piece = total_ref[d, p]
                    if step:
                        piece = pltpu.roll(piece, step % half_cols, 1)
                    value = piece if value is None else value + piece
            whole_ref[half_rows * p : half_rows * (p + 1), half_cols * odd : half_cols * (odd + 1)] = value
    for n in range(blocks):
        even = whole_ref[:, LANES * n : LANES * (n + 1)]
        odd = whole_ref[:, half_cols + LANES * n : half_cols + LANES * (n + 1)]
        block = split_rows(jnp.concatenate([even, odd], axis=1))
        grid_ref[:, 2 * LANES * n : 2 * LANES * (n + 1)] = dot(
            join_rows, dot(block, join).astype(jnp.bfloat16)
        )

    def landing(y, x):
        if x == 0:
            return end_ref.at[(y + 1) // 2]
        if y == 0:
            return side_ref.at[(x + 1) // 2]
        return corner_ref.at[(y + 1) + (x + 1) // 2]

    def fold_copy(n, y, x):
        return pltpu.make_async_remote_copy(
            src_ref=grid_ref.at[row_part(y), col_part(x)],
            dst_ref=landing(-y, -x),
            send_sem=fold_send.at[n],
            recv_sem=fold_recv.at[n],
            device_id=device(y, x),
            device_id_type=pl.DeviceIdType.MESH,
        )

    for n, (y, x) in enumerate(NEIGHBOURS):

        @pl.when(exists(y, x))
        def _():
            fold_copy(n, y, x).start()

    scale = 1.0 / float(visits) ** 0.5
    out_ref[...] += scale * grid_ref[ROWS : ROWS + height, 0:width]
    for n, (y, x) in enumerate(NEIGHBOURS):

        @pl.when(exists(-y, -x))
        def _():
            fold_copy(n, y, x).wait_recv()
            part = edge_of(-y, -x)
            out_ref[part] += scale * landing(-y, -x)[...]

    for n, (y, x) in enumerate(NEIGHBOURS):

        @pl.when(exists(y, x))
        def _():
            halo_copy(n, y, x).wait_send()
            fold_copy(n, y, x).wait_send()

    def sent(o, carry):
        frame_copy(o).wait_send()
        return carry

    lax.fori_loop(1, visit_count, sent, 0)


def solution(mesh):
    in_specs = (
        P(("tiles", "sky"), "visit"),
        P(("tiles", "visit"), "sky", None),
        P("tiles", None),
        P("tiles", None),
        P("tiles", None),
        P("tiles", None),
        P("tiles"),
    )
    out_specs = P(("tiles", "sky"), "visit")
    sky_count, visit_count = mesh.shape["sky"], mesh.shape["visit"]

    def on_device(sky_model, frames, psf_rows, psf_cols, dither, footprint, huber_cut):
        height, width = sky_model.shape
        per_device, low_rows = frames.shape[:2]
        low_cols = frames.shape[2] // visit_count
        half_rows, half_cols = height // 2 + ROWS, width // 2 + LANES
        f32 = jnp.float32
        return pl.pallas_call(
            functools.partial(kernel, (sky_count, visit_count)),
            out_shape=jax.ShapeDtypeStruct((height, width), f32),
            in_specs=[pl.BlockSpec(memory_space=pl.ANY)] * 2
            + [pl.BlockSpec(memory_space=pltpu.SMEM)] * 5,
            out_specs=pl.BlockSpec(memory_space=pltpu.VMEM),
            scratch_shapes=[
                pltpu.VMEM((height + 2 * ROWS, width + 2 * LANES), f32),
                pltpu.VMEM((SHIFTS, 2, half_rows, low_cols), f32),
                pltpu.VMEM((visit_count, per_device, low_rows, low_cols), jnp.bfloat16),
                pltpu.VMEM((2, half_rows, low_cols), f32),
                pltpu.VMEM((low_rows + 16, low_cols), f32),
                pltpu.VMEM((per_device, 2, half_rows, low_cols), f32),
                pltpu.VMEM((SHIFTS, 2, half_rows, half_cols), f32),
                pltpu.VMEM((height + 2 * ROWS, width + 2 * LANES), f32),
                pltpu.VMEM((2, height, LANES), f32),
                pltpu.VMEM((2, ROWS, width), f32),
                pltpu.VMEM((4, ROWS, LANES), f32),
                pltpu.SemaphoreType.DMA((2,)),
                pltpu.SemaphoreType.DMA((8,)),
                pltpu.SemaphoreType.DMA((8,)),
                pltpu.SemaphoreType.DMA((visit_count,)),
                pltpu.SemaphoreType.DMA((visit_count,)),
                pltpu.SemaphoreType.DMA((8,)),
                pltpu.SemaphoreType.DMA((8,)),
            ],
            compiler_params=pltpu.CompilerParams(
                collective_id=0, has_side_effects=True, vmem_limit_bytes=32 * 1024 * 1024
            ),
        )(sky_model, frames, psf_rows, psf_cols, dither, footprint, huber_cut)

    return jax.shard_map(
        on_device, mesh=mesh, in_specs=in_specs, out_specs=out_specs, check_vma=False
    )
```

```python
import functools

import jax
import jax.numpy as jnp
from jax import lax
from jax.experimental import pallas as pl
from jax.experimental.pallas import tpu as pltpu
from jax.sharding import PartitionSpec as P

TAPS = 5
REACH = 4
SHIFTS = 2 * REACH + 1

eps_flux = 0.1
tv_weight = 0.5

ROWS = 8
LANES = 128

NEIGHBOURS = tuple((y, x) for y in (-1, 0, 1) for x in (-1, 0, 1) if (y, x) != (0, 0))


def split_rows(value):
    high = value.astype(jnp.bfloat16)
    low = (value - high.astype(jnp.float32)).astype(jnp.bfloat16)
    return jnp.concatenate([high, low], axis=0)


def selection(shape, source_of):
    row = lax.broadcasted_iota(jnp.int32, shape, 0)
    col = lax.broadcasted_iota(jnp.int32, shape, 1)
    return jnp.where(source_of(row, col), 1.0, 0.0).astype(jnp.bfloat16)


def dot(a, b):
    return jnp.dot(a, b, preferred_element_type=jnp.float32)


def kernel(
    counts,
    model_ref,
    frames_ref,
    rows_in,
    cols_in,
    dither_in,
    footprint_in,
    cut_in,
    out_ref,
    rows_ref,
    cols_ref,
    dither_ref,
    footprint_ref,
    cut_ref,
    row_taps,
    col_taps,
    grid_ref,
    shifted_ref,
    frame_ref,
    blurred_ref,
    clipped_ref,
    back_ref,
    total_ref,
    whole_ref,
    side_ref,
    end_ref,
    corner_ref,
    local_sem,
    small_sem,
    halo_send,
    halo_recv,
    frame_send,
    frame_recv,
    fold_send,
    fold_recv,
):
    sky_count, visit_count = counts
    height, width = out_ref.shape
    per_device, low_rows, low_cols = frame_ref.shape[1:]
    visits = rows_ref.shape[0]
    full_rows, full_cols = grid_ref.shape
    half_rows, half_cols = full_rows // 2, full_cols // 2
    blocks = full_cols // (2 * LANES)
    tile = lax.axis_index("tiles")
    sky = lax.axis_index("sky")
    visit = lax.axis_index("visit")

    def device(y, x):
        return (tile, sky + y, visit + x)

    def exists(y, x):
        ok = None
        for step, at, count in ((y, sky, sky_count), (x, visit, visit_count)):
            if step:
                here = at > 0 if step < 0 else at < count - 1
                ok = here if ok is None else ok & here
        return ok

    def peer_of(o):
        return lax.rem(visit + o, visit_count)

    def row_part(y):
        return (pl.ds(0, ROWS), pl.ds(ROWS, height), pl.ds(ROWS + height, ROWS))[y + 1]

    def col_part(x):
        return (pl.ds(width + LANES, LANES), pl.ds(0, width), pl.ds(width, LANES))[x + 1]

    def edge_of(y, x):
        r = (pl.ds(0, ROWS), pl.ds(0, height), pl.ds(height - ROWS, ROWS))[y + 1]
        c = (pl.ds(0, LANES), pl.ds(0, width), pl.ds(width - LANES, LANES))[x + 1]
        return r, c

    barrier = pltpu.get_barrier_semaphore()

    def greet(o, carry):
        pl.semaphore_signal(
            barrier, inc=1, device_id=(tile, sky, peer_of(o)), device_id_type=pl.DeviceIdType.MESH
        )
        return carry

    lax.fori_loop(1, visit_count, greet, 0)
    for y, x in NEIGHBOURS:
        if y:

            @pl.when(exists(y, x))
            def _():
                pl.semaphore_signal(
                    barrier, inc=1, device_id=device(y, x), device_id_type=pl.DeviceIdType.MESH
                )

    small = [
        pltpu.make_async_copy(source, target, small_sem.at[n])
        for n, (source, target) in enumerate(
            (
                (rows_in, rows_ref),
                (cols_in, cols_ref),
                (dither_in, dither_ref),
                (footprint_in, footprint_ref),
                (cut_in, cut_ref),
            )
        )
    ]
    for copy in small:
        copy.start()
    own_model = pltpu.make_async_copy(
        model_ref, grid_ref.at[pl.ds(ROWS, height), pl.ds(0, width)], local_sem.at[0]
    )
    own_model.start()

    def own_frames():
        return pltpu.make_async_copy(
            frames_ref.at[:, :, pl.ds(pl.multiple_of(visit * low_cols, low_cols), low_cols)],
            frame_ref.at[0],
            local_sem.at[1],
        )

    own_frames().start()

    for copy in small:
        copy.wait()

    def place(k, carry):
        for ref, offset, placed in ((rows_ref, dither_ref[0, k], row_taps), (cols_ref, dither_ref[1, k], col_taps)):
            for d in range(SHIFTS):
                at = d - REACH - offset + TAPS // 2
                value = ref[k, jnp.clip(at, 0, TAPS - 1)]
                placed[k, d] = jnp.where((at >= 0) & (at < TAPS), value, 0.0)
        return carry

    lax.fori_loop(0, visits, place, 0)

    up, down = (sky > 0).astype(jnp.int32), (sky < sky_count - 1).astype(jnp.int32)
    left, right = (visit > 0).astype(jnp.int32), (visit < visit_count - 1).astype(jnp.int32)
    pl.semaphore_wait(barrier, visit_count - 1 + (up + down) * (1 + left + right))

    def halo_copy(n, y, x):
        return pltpu.make_async_remote_copy(
            src_ref=model_ref.at[edge_of(y, x)],
            dst_ref=grid_ref.at[row_part(-y), col_part(-x)],
            send_sem=halo_send.at[n],
            recv_sem=halo_recv.at[n],
            device_id=device(y, x),
            device_id_type=pl.DeviceIdType.MESH,
        )

    def frame_copy(o):
        peer = peer_of(o)
        return pltpu.make_async_remote_copy(
            src_ref=frames_ref.at[:, :, pl.ds(pl.multiple_of(peer * low_cols, low_cols), low_cols)],
            dst_ref=frame_ref.at[o],
            send_sem=frame_send.at[o],
            recv_sem=frame_recv.at[o],
            device_id=(tile, sky, peer),
            device_id_type=pl.DeviceIdType.MESH,
        )

    for n, (y, x) in enumerate(NEIGHBOURS):

        @pl.when(exists(y, x))
        def _():
            halo_copy(n, y, x).start()

    def send_frames(o, carry):
        frame_copy(o).start()
        return carry

    lax.fori_loop(1, visit_count, send_frames, 0)

    for y, x in NEIGHBOURS:

        @pl.when(jnp.logical_not(exists(y, x)))
        def _():
            part = (row_part(y), col_part(x))
            grid_ref[part] = jnp.zeros(grid_ref.at[part].shape, jnp.float32)

    margin = (clipped_ref.shape[0] - low_rows) // 2
    clipped_ref[0:margin, :] = jnp.zeros((margin, low_cols), jnp.float32)
    clipped_ref[margin + low_rows :, :] = jnp.zeros((margin, low_cols), jnp.float32)
    total_ref[...] = jnp.zeros(total_ref.shape, jnp.float32)
    spread = selection(
        (2 * LANES, 2 * LANES),
        lambda a, b: a == jnp.where(b < LANES, 2 * b, 2 * b - (2 * LANES - 1)),
    )
    join = selection(
        (2 * LANES, 2 * LANES),
        lambda a, b: b == jnp.where(a < LANES, 2 * a, 2 * a - (2 * LANES - 1)),
    )

    def folded(b):
        return jnp.where(b >= full_rows, b - full_rows, b)

    part_rows = selection(
        (full_rows, 2 * full_rows),
        lambda a, b: folded(b) == jnp.where(a < half_rows, 2 * a, 2 * a - (full_rows - 1)),
    )
    join_rows = selection(
        (full_rows, 2 * full_rows),
        lambda a, b: a == jnp.where(folded(b) < half_rows, 2 * folded(b), 2 * folded(b) - (full_rows - 1)),
    )

    own_model.wait()
    for n, (y, x) in enumerate(NEIGHBOURS):
        @pl.when(exists(-y, -x))
        def _():
            halo_copy(n, y, x).wait_recv()

    for n in range(blocks):
        block = split_rows(grid_ref[:, 2 * LANES * n : 2 * LANES * (n + 1)])
        apart = dot(part_rows, dot(block, spread).astype(jnp.bfloat16))
        whole_ref[:, LANES * n : LANES * (n + 1)] = apart[:, :LANES]
        whole_ref[:, half_cols + LANES * n : half_cols + LANES * (n + 1)] = apart[:, LANES:]
    for d in range(SHIFTS):
        odd, step = (d - REACH) % 2, (d - REACH) // 2
        for p in range(2):
            value = whole_ref[half_rows * p : half_rows * (p + 1), half_cols * odd : half_cols * (odd + 1)]
            if step:
                value = pltpu.roll(value, (-step) % half_cols, 1)
            shifted_ref[d, p] = value[:, :low_cols]

    strip = 16

    def next_col(value):
        return pltpu.roll(value, full_cols - 1, 1)

    for t in range(height // strip):
        above = grid_ref[ROWS - 1 + strip * t : ROWS - 1 + strip * (t + 1), :]
        here = grid_ref[ROWS + strip * t : ROWS + strip * (t + 1), :]
        below = grid_ref[ROWS + 1 + strip * t : ROWS + 1 + strip * (t + 1), :]
        gx, gy = here - above, next_col(above) - above
        value = gx * lax.rsqrt(gx * gx + gy * gy + eps_flux)
        gx, gy = below - here, next_col(here) - here
        scale = lax.rsqrt(gx * gx + gy * gy + eps_flux)
        flux = gy * scale
        value = value - gx * scale + (pltpu.roll(flux, 1, 1) - flux)
        out_ref[strip * t : strip * (t + 1), :] = tv_weight * value[:, :width]

    own_frames().wait()
    low_index = sky * low_rows + lax.broadcasted_iota(jnp.int32, (low_rows, low_cols), 0)

    def chunk(o, carry):
        @pl.when(o > 0)
        def _():
            frame_copy(o).wait_recv()

        owner = lax.rem(visit - o + visit_count, visit_count)
        for j in range(per_device):
            k = owner * per_device + j
            col_shift = dither_ref[1, k]
            for p in range(2):
                value = None
                for b in range(TAPS):
                    piece = cols_ref[k, b] * shifted_ref[col_shift + (b - TAPS // 2 + REACH), p]
                    value = piece if value is None else value + piece
                blurred_ref[p] = value
            predicted = None
            for d in range(SHIFTS):
                odd, step = (d - REACH) % 2, (d - REACH) // 2
                begin = ROWS // 2 + step
                piece = row_taps[k, d] * blurred_ref[odd, begin : begin + low_rows, :]
                predicted = piece if predicted is None else predicted + piece
            cut = cut_ref[k]
            inside = (low_index >= footprint_ref[0, k]) & (low_index < footprint_ref[1, k])
            error = predicted - frame_ref[o, j].astype(jnp.float32)
            clipped_ref[margin : margin + low_rows, :] = jnp.where(
                inside, jnp.minimum(jnp.maximum(error, -cut), cut), 0.0
            )
            for p in range(2):
                value = None
                for d in range(SHIFTS):
                    odd, step = (d - REACH) % 2, (d - REACH) // 2
                    if odd == p:
                        begin = margin - ROWS // 2 - step
                        piece = row_taps[k, d] * clipped_ref[begin : begin + half_rows, :]
                        value = piece if value is None else value + piece
                back_ref[j, p] = value
        weights = [
            [col_taps[owner * per_device + j, d] for d in range(SHIFTS)] for j in range(per_device)
        ]
        for p in range(2):
            for t in range(half_rows // 8):
                rows = slice(8 * t, 8 * (t + 1))
                back = [back_ref[j, p, rows] for j in range(per_device)]
                for d in range(SHIFTS):
                    value = total_ref[d, p, rows, :low_cols]
                    for j in range(per_device):
                        value = value + weights[j][d] * back[j]
                    total_ref[d, p, rows, :low_cols] = value
        return carry

    lax.fori_loop(0, visit_count, chunk, 0)

    for odd in range(2):
        for p in range(2):
            value = None
            for d in range(SHIFTS):
                step = (d - REACH) // 2
                if (d - REACH) % 2 == odd:
                    piece = total_ref[d, p]
                    if step:
                        piece = pltpu.roll(piece, step % half_cols, 1)
                    value = piece if value is None else value + piece
            whole_ref[half_rows * p : half_rows * (p + 1), half_cols * odd : half_cols * (odd + 1)] = value
    def landing(y, x):
        if x == 0:
            return end_ref.at[(y + 1) // 2]
        if y == 0:
            return side_ref.at[(x + 1) // 2]
        return corner_ref.at[(y + 1) + (x + 1) // 2]

    def fold_copy(n, y, x):
        return pltpu.make_async_remote_copy(
            src_ref=grid_ref.at[row_part(y), col_part(x)],
            dst_ref=landing(-y, -x),
            send_sem=fold_send.at[n],
            recv_sem=fold_recv.at[n],
            device_id=device(y, x),
            device_id_type=pl.DeviceIdType.MESH,
        )

    def fold_start(beside):
        for n, (y, x) in enumerate(NEIGHBOURS):
            if (x != 0) == beside:

                @pl.when(exists(y, x))
                def _():
                    fold_copy(n, y, x).start()

    for n in reversed(range(blocks)):
        even = whole_ref[:, LANES * n : LANES * (n + 1)]
        odd = whole_ref[:, half_cols + LANES * n : half_cols + LANES * (n + 1)]
        block = split_rows(jnp.concatenate([even, odd], axis=1))
        grid_ref[:, 2 * LANES * n : 2 * LANES * (n + 1)] = dot(
            join_rows, dot(block, join).astype(jnp.bfloat16)
        )
        if n == blocks - 1:
            fold_start(True)
    fold_start(False)

    scale = 1.0 / float(visits) ** 0.5
    out_ref[...] += scale * grid_ref[ROWS : ROWS + height, 0:width]
    for n, (y, x) in enumerate(NEIGHBOURS):

        @pl.when(exists(-y, -x))
        def _():
            fold_copy(n, y, x).wait_recv()
            part = edge_of(-y, -x)
            out_ref[part] += scale * landing(-y, -x)[...]

    for n, (y, x) in enumerate(NEIGHBOURS):

        @pl.when(exists(y, x))
        def _():
            halo_copy(n, y, x).wait_send()
            fold_copy(n, y, x).wait_send()

    def sent(o, carry):
        frame_copy(o).wait_send()
        return carry

    lax.fori_loop(1, visit_count, sent, 0)


def solution(mesh):
    in_specs = (
        P(("tiles", "sky"), "visit"),
        P(("tiles", "visit"), "sky", None),
        P("tiles", None),
        P("tiles", None),
        P("tiles", None),
        P("tiles", None),
        P("tiles"),
    )
    out_specs = P(("tiles", "sky"), "visit")
    sky_count, visit_count = mesh.shape["sky"], mesh.shape["visit"]

    def on_device(sky_model, frames, psf_rows, psf_cols, dither, footprint, huber_cut):
        height, width = sky_model.shape
        per_device, low_rows = frames.shape[:2]
        visits = psf_rows.shape[0]
        low_cols = frames.shape[2] // visit_count
        half_rows, half_cols = height // 2 + ROWS, width // 2 + LANES
        f32 = jnp.float32
        return pl.pallas_call(
            functools.partial(kernel, (sky_count, visit_count)),
            out_shape=jax.ShapeDtypeStruct((height, width), f32),
            in_specs=[pl.BlockSpec(memory_space=pltpu.HBM)] * 7,
            out_specs=pl.BlockSpec(memory_space=pltpu.VMEM),
            scratch_shapes=[
                pltpu.SMEM(psf_rows.shape, f32),
                pltpu.SMEM(psf_cols.shape, f32),
                pltpu.SMEM(dither.shape[::-1], jnp.int32),
                pltpu.SMEM(footprint.shape[::-1], jnp.int32),
                pltpu.SMEM(huber_cut.shape, f32),
                pltpu.SMEM((visits, SHIFTS), f32),
                pltpu.SMEM((visits, SHIFTS), f32),
                pltpu.VMEM((height + 2 * ROWS, width + 2 * LANES), f32),
                pltpu.VMEM((SHIFTS, 2, half_rows, low_cols), f32),
                pltpu.VMEM((visit_count, per_device, low_rows, low_cols), jnp.bfloat16),
                pltpu.VMEM((2, half_rows, low_cols), f32),
                pltpu.VMEM((low_rows + 16, low_cols), f32),
                pltpu.VMEM((per_device, 2, half_rows, low_cols), f32),
                pltpu.VMEM((SHIFTS, 2, half_rows, half_cols), f32),
                pltpu.VMEM((height + 2 * ROWS, width + 2 * LANES), f32),
                pltpu.VMEM((2, height, LANES), f32),
                pltpu.VMEM((2, ROWS, width), f32),
                pltpu.VMEM((4, ROWS, LANES), f32),
                pltpu.SemaphoreType.DMA((2,)),
                pltpu.SemaphoreType.DMA((5,)),
                pltpu.SemaphoreType.DMA((8,)),
                pltpu.SemaphoreType.DMA((8,)),
                pltpu.SemaphoreType.DMA((visit_count,)),
                pltpu.SemaphoreType.DMA((visit_count,)),
                pltpu.SemaphoreType.DMA((8,)),
                pltpu.SemaphoreType.DMA((8,)),
            ],
            compiler_params=pltpu.CompilerParams(
                collective_id=0, has_side_effects=True, vmem_limit_bytes=63 * 1024 * 1024
            ),
        )(sky_model, frames, psf_rows, psf_cols, dither.T, footprint.T, huber_cut)

    return jax.shard_map(
        on_device, mesh=mesh, in_specs=in_specs, out_specs=out_specs, check_vma=False
    )
```

```python
import functools

import jax
import jax.numpy as jnp
from jax import lax
from jax.experimental import pallas as pl
from jax.experimental.pallas import tpu as pltpu
from jax.sharding import PartitionSpec as P

TAPS = 5
REACH = 4
SHIFTS = 2 * REACH + 1

eps_flux = 0.1
tv_weight = 0.5

ROWS = 8
LANES = 128

NEIGHBOURS = tuple((y, x) for y in (-1, 0, 1) for x in (-1, 0, 1) if (y, x) != (0, 0))


def split_rows(value):
    high = value.astype(jnp.bfloat16)
    low = (value - high.astype(jnp.float32)).astype(jnp.bfloat16)
    return jnp.concatenate([high, low], axis=0)


def selection(shape, source_of):
    row = lax.broadcasted_iota(jnp.int32, shape, 0)
    col = lax.broadcasted_iota(jnp.int32, shape, 1)
    return jnp.where(source_of(row, col), 1.0, 0.0).astype(jnp.bfloat16)


def dot(a, b):
    return jnp.dot(a, b, preferred_element_type=jnp.float32)


def kernel(
    counts,
    model_ref,
    frames_ref,
    rows_in,
    cols_in,
    dither_in,
    footprint_in,
    cut_in,
    out_ref,
    rows_ref,
    cols_ref,
    dither_ref,
    footprint_ref,
    cut_ref,
    row_taps,
    col_taps,
    grid_ref,
    shifted_ref,
    frame_ref,
    blurred_ref,
    clipped_ref,
    back_ref,
    total_ref,
    whole_ref,
    sum_ref,
    side_out,
    side_in,
    side_ref,
    end_ref,
    corner_ref,
    local_sem,
    small_sem,
    halo_send,
    halo_recv,
    frame_send,
    frame_recv,
    fold_send,
    fold_recv,
):
    sky_count, visit_count = counts
    height, width = out_ref.shape
    per_device, low_rows, low_cols = frame_ref.shape[1:]
    visits = rows_ref.shape[0]
    full_rows, full_cols = grid_ref.shape
    half_rows, half_cols = full_rows // 2, full_cols // 2
    blocks = full_cols // (2 * LANES)
    tile = lax.axis_index("tiles")
    sky = lax.axis_index("sky")
    visit = lax.axis_index("visit")

    def device(y, x):
        return (tile, sky + y, visit + x)

    def exists(y, x):
        ok = None
        for step, at, count in ((y, sky, sky_count), (x, visit, visit_count)):
            if step:
                here = at > 0 if step < 0 else at < count - 1
                ok = here if ok is None else ok & here
        return ok

    def peer_of(o):
        return lax.rem(visit + o, visit_count)

    def row_part(y):
        return (pl.ds(0, ROWS), pl.ds(ROWS, height), pl.ds(ROWS + height, ROWS))[y + 1]

    def col_part(x):
        return (pl.ds(width + LANES, LANES), pl.ds(0, width), pl.ds(width, LANES))[x + 1]

    def edge_of(y, x):
        r = (pl.ds(0, ROWS), pl.ds(0, height), pl.ds(height - ROWS, ROWS))[y + 1]
        c = (pl.ds(0, LANES), pl.ds(0, width), pl.ds(width - LANES, LANES))[x + 1]
        return r, c

    barrier = pltpu.get_barrier_semaphore()

    def greet(o, carry):
        pl.semaphore_signal(
            barrier, inc=1, device_id=(tile, sky, peer_of(o)), device_id_type=pl.DeviceIdType.MESH
        )
        return carry

    lax.fori_loop(1, visit_count, greet, 0)
    for y, x in NEIGHBOURS:
        if y:

            @pl.when(exists(y, x))
            def _():
                pl.semaphore_signal(
                    barrier, inc=1, device_id=device(y, x), device_id_type=pl.DeviceIdType.MESH
                )

    small = [
        pltpu.make_async_copy(source, target, small_sem.at[n])
        for n, (source, target) in enumerate(
            (
                (rows_in, rows_ref),
                (cols_in, cols_ref),
                (dither_in, dither_ref),
                (footprint_in, footprint_ref),
                (cut_in, cut_ref),
            )
        )
    ]
    for copy in small:
        copy.start()
    own_model = pltpu.make_async_copy(
        model_ref, grid_ref.at[pl.ds(ROWS, height), pl.ds(0, width)], local_sem.at[0]
    )
    own_model.start()

    def own_frames():
        return pltpu.make_async_copy(
            frames_ref.at[:, :, pl.ds(pl.multiple_of(visit * low_cols, low_cols), low_cols)],
            frame_ref.at[0],
            local_sem.at[1],
        )

    own_frames().start()

    for copy in small:
        copy.wait()

    def place(k, carry):
        for ref, offset, placed in ((rows_ref, dither_ref[0, k], row_taps), (cols_ref, dither_ref[1, k], col_taps)):
            for d in range(SHIFTS):
                at = d - REACH - offset + TAPS // 2
                value = ref[k, jnp.clip(at, 0, TAPS - 1)]
                placed[k, d] = jnp.where((at >= 0) & (at < TAPS), value, 0.0)
        return carry

    lax.fori_loop(0, visits, place, 0)

    lane = lax.broadcasted_iota(jnp.int32, (8, LANES), 1)
    own_model.wait()
    for side in range(2):
        packed = jnp.zeros((8, LANES), jnp.float32)
        begin = (width - LANES) * side
        for t in range(height // 8):
            piece = grid_ref[ROWS + 8 * t : ROWS + 8 * (t + 1), begin : begin + LANES]
            shift = (8 * t + 8 * side) % LANES
            piece = pltpu.roll(piece, shift, 1) if shift else piece
            packed = jnp.where((lane >= 8 * t) & (lane < 8 * t + 8), piece, packed)
        side_out[side] = packed

    up, down = (sky > 0).astype(jnp.int32), (sky < sky_count - 1).astype(jnp.int32)
    left, right = (visit > 0).astype(jnp.int32), (visit < visit_count - 1).astype(jnp.int32)
    pl.semaphore_wait(barrier, visit_count - 1 + (up + down) * (1 + left + right))

    def halo_copy(n, y, x):
        if y == 0:
            side = (x + 1) // 2
            return pltpu.make_async_remote_copy(
                src_ref=side_out.at[side],
                dst_ref=side_in.at[side],
                send_sem=halo_send.at[n],
                recv_sem=halo_recv.at[n],
                device_id=device(y, x),
                device_id_type=pl.DeviceIdType.MESH,
            )
        return pltpu.make_async_remote_copy(
            src_ref=model_ref.at[edge_of(y, x)],
            dst_ref=grid_ref.at[row_part(-y), col_part(-x)],
            send_sem=halo_send.at[n],
            recv_sem=halo_recv.at[n],
            device_id=device(y, x),
            device_id_type=pl.DeviceIdType.MESH,
        )

    def frame_copy(o):
        peer = peer_of(o)
        return pltpu.make_async_remote_copy(
            src_ref=frames_ref.at[:, :, pl.ds(pl.multiple_of(peer * low_cols, low_cols), low_cols)],
            dst_ref=frame_ref.at[o],
            send_sem=frame_send.at[o],
            recv_sem=frame_recv.at[o],
            device_id=(tile, sky, peer),
            device_id_type=pl.DeviceIdType.MESH,
        )

    for n, (y, x) in enumerate(NEIGHBOURS):

        @pl.when(exists(y, x))
        def _():
            halo_copy(n, y, x).start()

    def send_frames(o, carry):
        frame_copy(o).start()
        return carry

    lax.fori_loop(1, visit_count, send_frames, 0)

    for y, x in NEIGHBOURS:

        @pl.when(jnp.logical_not(exists(y, x)))
        def _():
            part = (row_part(y), col_part(x))
            grid_ref[part] = jnp.zeros(grid_ref.at[part].shape, jnp.float32)

    margin = (clipped_ref.shape[0] - low_rows) // 2
    clipped_ref[0:margin, :] = jnp.zeros((margin, low_cols), jnp.float32)
    clipped_ref[margin + low_rows :, :] = jnp.zeros((margin, low_cols), jnp.float32)
    total_ref[...] = jnp.zeros(total_ref.shape, jnp.float32)
    spread = selection(
        (2 * LANES, 2 * LANES),
        lambda a, b: a == jnp.where(b < LANES, 2 * b, 2 * b - (2 * LANES - 1)),
    )
    join = selection(
        (2 * LANES, 2 * LANES),
        lambda a, b: b == jnp.where(a < LANES, 2 * a, 2 * a - (2 * LANES - 1)),
    )

    def folded(b):
        return jnp.where(b >= full_rows, b - full_rows, b)

    part_rows = selection(
        (full_rows, 2 * full_rows),
        lambda a, b: folded(b) == jnp.where(a < half_rows, 2 * a, 2 * a - (full_rows - 1)),
    )
    join_rows = selection(
        (full_rows, 2 * full_rows),
        lambda a, b: a == jnp.where(folded(b) < half_rows, 2 * folded(b), 2 * folded(b) - (full_rows - 1)),
    )

    for n, (y, x) in enumerate(NEIGHBOURS):
        @pl.when(exists(-y, -x))
        def _():
            halo_copy(n, y, x).wait_recv()
            if y == 0:
                side = (x + 1) // 2
                packed = side_in[side]
                begin = width + LANES * side
                for t in range(height // 8):
                    shift = (-8 * t - 8 * side) % LANES
                    piece = pltpu.roll(packed, shift, 1) if shift else packed
                    keep = lane >= LANES - 8 if side else lane < 8
                    grid_ref[ROWS + 8 * t : ROWS + 8 * (t + 1), begin : begin + LANES] = jnp.where(
                        keep, piece, 0.0
                    )

    for n in range(blocks):
        block = split_rows(grid_ref[:, 2 * LANES * n : 2 * LANES * (n + 1)])
        apart = dot(part_rows, dot(block, spread).astype(jnp.bfloat16))
        whole_ref[:, LANES * n : LANES * (n + 1)] = apart[:, :LANES]
        whole_ref[:, half_cols + LANES * n : half_cols + LANES * (n + 1)] = apart[:, LANES:]
    for d in range(SHIFTS):
        odd, step = (d - REACH) % 2, (d - REACH) // 2
        for p in range(2):
            value = whole_ref[half_rows * p : half_rows * (p + 1), half_cols * odd : half_cols * (odd + 1)]
            if step:
                value = pltpu.roll(value, (-step) % half_cols, 1)
            shifted_ref[d, p] = value[:, :low_cols]

    own_frames().wait()
    low_index = sky * low_rows + lax.broadcasted_iota(jnp.int32, (low_rows, low_cols), 0)

    def chunk(o, carry):
        @pl.when(o > 0)
        def _():
            frame_copy(o).wait_recv()

        owner = lax.rem(visit - o + visit_count, visit_count)
        for j in range(per_device):
            k = owner * per_device + j
            col_shift = dither_ref[1, k]
            for p in range(2):
                value = None
                for b in range(TAPS):
                    piece = cols_ref[k, b] * shifted_ref[col_shift + (b - TAPS // 2 + REACH), p]
                    value = piece if value is None else value + piece
                blurred_ref[p] = value
            predicted = None
            for d in range(SHIFTS):
                odd, step = (d - REACH) % 2, (d - REACH) // 2
                begin = ROWS // 2 + step
                piece = row_taps[k, d] * blurred_ref[odd, begin : begin + low_rows, :]
                predicted = piece if predicted is None else predicted + piece
            cut = cut_ref[k]
            inside = (low_index >= footprint_ref[0, k]) & (low_index < footprint_ref[1, k])
            error = predicted - frame_ref[o, j].astype(jnp.float32)
            clipped_ref[margin : margin + low_rows, :] = jnp.where(
                inside, jnp.minimum(jnp.maximum(error, -cut), cut), 0.0
            )
            for p in range(2):
                value = None
                for d in range(SHIFTS):
                    odd, step = (d - REACH) % 2, (d - REACH) // 2
                    if odd == p:
                        begin = margin - ROWS // 2 - step
                        piece = row_taps[k, d] * clipped_ref[begin : begin + half_rows, :]
                        value = piece if value is None else value + piece
                back_ref[j, p] = value
        weights = [
            [col_taps[owner * per_device + j, d] for d in range(SHIFTS)] for j in range(per_device)
        ]
        for p in range(2):
            for t in range(half_rows // 8):
                rows = slice(8 * t, 8 * (t + 1))
                back = [back_ref[j, p, rows] for j in range(per_device)]
                for d in range(SHIFTS):
                    value = total_ref[d, p, rows, :low_cols]
                    for j in range(per_device):
                        value = value + weights[j][d] * back[j]
                    total_ref[d, p, rows, :low_cols] = value
        return carry

    lax.fori_loop(0, visit_count, chunk, 0)

    for odd in range(2):
        for p in range(2):
            value = None
            for d in range(SHIFTS):
                step = (d - REACH) // 2
                if (d - REACH) % 2 == odd:
                    piece = total_ref[d, p]
                    if step:
                        piece = pltpu.roll(piece, step % half_cols, 1)
                    value = piece if value is None else value + piece
            whole_ref[half_rows * p : half_rows * (p + 1), half_cols * odd : half_cols * (odd + 1)] = value
    def landing(y, x):
        if x == 0:
            return end_ref.at[(y + 1) // 2]
        if y == 0:
            return side_ref.at[(x + 1) // 2]
        return corner_ref.at[(y + 1) + (x + 1) // 2]

    def fold_copy(n, y, x):
        return pltpu.make_async_remote_copy(
            src_ref=sum_ref.at[row_part(y), col_part(x)],
            dst_ref=landing(-y, -x),
            send_sem=fold_send.at[n],
            recv_sem=fold_recv.at[n],
            device_id=device(y, x),
            device_id_type=pl.DeviceIdType.MESH,
        )

    def fold_start(beside):
        for n, (y, x) in enumerate(NEIGHBOURS):
            if (x != 0) == beside:

                @pl.when(exists(y, x))
                def _():
                    fold_copy(n, y, x).start()

    for n in reversed(range(blocks)):
        even = whole_ref[:, LANES * n : LANES * (n + 1)]
        odd = whole_ref[:, half_cols + LANES * n : half_cols + LANES * (n + 1)]
        block = split_rows(jnp.concatenate([even, odd], axis=1))
        sum_ref[:, 2 * LANES * n : 2 * LANES * (n + 1)] = dot(
            join_rows, dot(block, join).astype(jnp.bfloat16)
        )
        if n == blocks - 1:
            fold_start(True)
    fold_start(False)

    share = 1.0 / float(visits) ** 0.5

    strip = 16

    def next_col(value):
        return pltpu.roll(value, full_cols - 1, 1)

    for t in range(height // strip):
        above = grid_ref[ROWS - 1 + strip * t : ROWS - 1 + strip * (t + 1), :]
        here = grid_ref[ROWS + strip * t : ROWS + strip * (t + 1), :]
        below = grid_ref[ROWS + 1 + strip * t : ROWS + 1 + strip * (t + 1), :]
        gx, gy = here - above, next_col(above) - above
        value = gx * lax.rsqrt(gx * gx + gy * gy + eps_flux)
        gx, gy = below - here, next_col(here) - here
        scale = lax.rsqrt(gx * gx + gy * gy + eps_flux)
        flux = gy * scale
        value = value - gx * scale + (pltpu.roll(flux, 1, 1) - flux)
        data = sum_ref[ROWS + strip * t : ROWS + strip * (t + 1), 0:width]
        out_ref[strip * t : strip * (t + 1), :] = share * data + tv_weight * value[:, :width]

    for n, (y, x) in enumerate(NEIGHBOURS):

        @pl.when(exists(-y, -x))
        def _():
            fold_copy(n, y, x).wait_recv()
            part = edge_of(-y, -x)
            out_ref[part] += share * landing(-y, -x)[...]

    for n, (y, x) in enumerate(NEIGHBOURS):

        @pl.when(exists(y, x))
        def _():
            halo_copy(n, y, x).wait_send()
            fold_copy(n, y, x).wait_send()

    def sent(o, carry):
        frame_copy(o).wait_send()
        return carry

    lax.fori_loop(1, visit_count, sent, 0)


def solution(mesh):
    in_specs = (
        P(("tiles", "sky"), "visit"),
        P(("tiles", "visit"), "sky", None),
        P("tiles", None),
        P("tiles", None),
        P("tiles", None),
        P("tiles", None),
        P("tiles"),
    )
    out_specs = P(("tiles", "sky"), "visit")
    sky_count, visit_count = mesh.shape["sky"], mesh.shape["visit"]

    def on_device(sky_model, frames, psf_rows, psf_cols, dither, footprint, huber_cut):
        height, width = sky_model.shape
        per_device, low_rows = frames.shape[:2]
        visits = psf_rows.shape[0]
        low_cols = frames.shape[2] // visit_count
        half_rows, half_cols = height // 2 + ROWS, width // 2 + LANES
        f32 = jnp.float32
        return pl.pallas_call(
            functools.partial(kernel, (sky_count, visit_count)),
            out_shape=jax.ShapeDtypeStruct((height, width), f32),
            in_specs=[pl.BlockSpec(memory_space=pltpu.HBM)] * 7,
            out_specs=pl.BlockSpec(memory_space=pltpu.VMEM),
            scratch_shapes=[
                pltpu.SMEM(psf_rows.shape, f32),
                pltpu.SMEM(psf_cols.shape, f32),
                pltpu.SMEM(dither.shape[::-1], jnp.int32),
                pltpu.SMEM(footprint.shape[::-1], jnp.int32),
                pltpu.SMEM(huber_cut.shape, f32),
                pltpu.SMEM((visits, SHIFTS), f32),
                pltpu.SMEM((visits, SHIFTS), f32),
                pltpu.VMEM((height + 2 * ROWS, width + 2 * LANES), f32),
                pltpu.VMEM((SHIFTS, 2, half_rows, low_cols), f32),
                pltpu.VMEM((visit_count, per_device, low_rows, low_cols), jnp.bfloat16),
                pltpu.VMEM((2, half_rows, low_cols), f32),
                pltpu.VMEM((low_rows + 16, low_cols), f32),
                pltpu.VMEM((per_device, 2, half_rows, low_cols), f32),
                pltpu.VMEM((SHIFTS, 2, half_rows, half_cols), f32),
                pltpu.VMEM((height + 2 * ROWS, width + 2 * LANES), f32),
                pltpu.VMEM((height + 2 * ROWS, width + 2 * LANES), f32),
                pltpu.VMEM((2, 8, LANES), f32),
                pltpu.VMEM((2, 8, LANES), f32),
                pltpu.VMEM((2, height, LANES), f32),
                pltpu.VMEM((2, ROWS, width), f32),
                pltpu.VMEM((4, ROWS, LANES), f32),
                pltpu.SemaphoreType.DMA((2,)),
                pltpu.SemaphoreType.DMA((5,)),
                pltpu.SemaphoreType.DMA((8,)),
                pltpu.SemaphoreType.DMA((8,)),
                pltpu.SemaphoreType.DMA((visit_count,)),
                pltpu.SemaphoreType.DMA((visit_count,)),
                pltpu.SemaphoreType.DMA((8,)),
                pltpu.SemaphoreType.DMA((8,)),
            ],
            compiler_params=pltpu.CompilerParams(
                collective_id=0, has_side_effects=True, vmem_limit_bytes=63 * 1024 * 1024
            ),
        )(sky_model, frames, psf_rows, psf_cols, dither.T, footprint.T, huber_cut)

    return jax.shard_map(
        on_device, mesh=mesh, in_specs=in_specs, out_specs=out_specs, check_vma=False
    )
```
